32 devices in a mesh: row: 4 (over y, core), col: 8 (over z, x).
Axes of the slice: x: 2, y: 2, z: 4, core: 2. Of those that a mesh axis runs over, the one named last changes fastest.
Arguments:
- matrix: float32 [32, 4, 128, 16, 8, 128], P(None, 'row', None, None, 'col'), may hold values from -8.5 to 8.5
- vectors: float32 [2, 32, 4, 128, 96], P(None, None, 'row', 'col'), may hold values from -0.046875 to 0.046875
- factors: float32 [2, 96, 96], replicated, may hold values from -0.30618622 to 1.6, as said below
Outputs:
- updated: float32 [32, 4, 128, 16, 8, 128], P(None, 'row', None, None, 'col')
The draws below stay inside these ranges and needn't reach their ends.
Inputs may be any that keep to these rules, and one draw needn't show every extreme that they name: Each factors[k] is upper triangular with a positive diagonal.
All inputs are finite; a program needn't handle non-finite values.
Results may differ from the reference program's by a relative error of at most 0.0001.
Values sent between devices are 32-bit elements; how exact they have to be, the bound alone decides.
A program may use at most 192 MiB of HBM per device.

```python
import math
import jax
import jax.numpy as jnp
from jax import lax

N = 16384
TB = 128
PW = 96
PANELS = 2
LT = 32
LC = 16
N_ROW = 4
N_COL = 8


def draw_matrix(key, part):
    random_part = jnp.clip(jax.random.normal(key, (N, N), jnp.float32), -6.0, 6.0)
    symmetric = (random_part + random_part.T) * 0.7071
    return symmetric.reshape(LT, N_ROW, TB, LC, N_COL, TB)


def draw_factors(key, part):
    first_key = jax.random.fold_in(key, 11)
    second_key = jax.random.fold_in(key, 12)
    upper = jnp.clip(jax.random.normal(first_key, (PANELS, PW, PW), jnp.float32), -6.0, 6.0) * (0.5 / math.sqrt(PW))
    diagonal = jax.random.uniform(second_key, (PANELS, PW), jnp.float32, 0.8, 1.6)
    strict = jnp.triu(jnp.ones((PW, PW), jnp.float32), 1)
    return upper * strict + diagonal[:, :, None] * jnp.eye(PW, dtype=jnp.float32)


def block_levels(own_key, dims, cuts, least, top_value):
    def one(axis_at, blocks):
        draws = jax.random.uniform(jax.random.fold_in(jax.random.fold_in(own_key, 6), axis_at), (blocks,), jnp.float32, least / len(cuts), top_value / len(cuts))
        return jnp.repeat(jnp.exp(draws), dims[axis_at] // blocks).reshape((-1,) + (1,) * (len(dims) - axis_at - 1))

    factor_of = one(*cuts[0])
    for cut in cuts[1:]:
        factor_of = factor_of * one(*cut)
    return factor_of


def gaussian(stream_key, dims, width, most, pieces=(), kind=jnp.bfloat16):
    values = jax.random.normal(stream_key, dims, jnp.float32) * width
    if len(pieces) > 0:
        values = block_levels(stream_key, dims, pieces, -0.22, 0.18) * values
    return jnp.clip(values, min=-most, max=most).astype(kind)


def setup_inputs(seed: int = 0) -> dict:
    key_of = jax.random.split(jax.random.key(seed), 4)
    return {
        "matrix": draw_matrix(jax.random.fold_in(key_of[3], 71), 0),
        "vectors": gaussian(key_of[1], (PANELS, LT, N_ROW, TB, PW), N ** -0.5, 0.046875, ((2, 4), (3, 8)), jnp.float32),
        "factors": draw_factors(jax.random.fold_in(key_of[3], 71), 0),
    }


def product(matrix_a, matrix_b):
    return jnp.dot(matrix_a, matrix_b, precision=lax.Precision.HIGHEST, preferred_element_type=jnp.float32)


def reference(matrix, vectors, factors):
    current = matrix.reshape(N, N)
    for number in range(PANELS):
        basis = vectors[number].reshape(N, PW)
        factor = factors[number]
        update = product(product(current, basis), factor)
        correlation = product(basis.T, update)
        update = update - 0.5 * product(basis, product(factor.T, correlation))
        current = current - product(basis, update.T) - product(update, basis.T)
    return current.reshape(matrix.shape)
```

```python
import jax
import jax.numpy as jnp
from jax import lax
from jax.sharding import PartitionSpec as P


def spread(array, axis, root):
    mine = lax.axis_index(axis) == root
    return lax.psum(jnp.where(mine, array, jnp.zeros_like(array)), axis)


def product(matrix_a, matrix_b):
    return jnp.dot(
        matrix_a, matrix_b, precision=lax.Precision.HIGHEST, preferred_element_type=jnp.float32
    )


def large_product(matrix_a, matrix_b):
    return jnp.dot(
        matrix_a, matrix_b, precision=lax.Precision.HIGH, preferred_element_type=jnp.float32
    )


def contract(matrix_a, matrix_b):
    return lax.dot_general(
        matrix_a,
        matrix_b,
        (((0,), (0,)), ((), ())),
        precision=lax.Precision.HIGH,
        preferred_element_type=jnp.float32,
    )


def select_cols(rows, col_tiles, stride, parity):
    width = rows.shape[-1]
    tile_size = rows.shape[-2] // (col_tiles * stride)
    shaped = rows.reshape(rows.shape[:-2] + (col_tiles, stride, tile_size, width))
    axis_at = len(rows.shape) - 1
    picked = lax.dynamic_index_in_dim(shaped, parity, axis_at, keepdims=False)
    return picked.reshape(rows.shape[:-2] + (col_tiles * tile_size, width))


def rank_update(blocks, rows_left, update_rows, update_cols, cols_right):
    left_side = jnp.concatenate([rows_left, update_rows], axis=1)
    right_side = jnp.concatenate([update_cols, cols_right], axis=1)
    return blocks - lax.dot_general(
        left_side,
        right_side,
        (((1,), (1,)), ((), ())),
        precision=lax.Precision.HIGH,
        preferred_element_type=jnp.float32,
    )


def shards(matrix, vectors, factors):
    row_tiles, tile_size, col_tiles = (matrix.shape[0], matrix.shape[2], matrix.shape[3])
    panel_count, width = (factors.shape[0], factors.shape[1])
    n_rows = lax.axis_size("row")
    n_cols = lax.axis_size("col")
    stride = n_cols // n_rows
    col_index = lax.axis_index("col")
    source = col_index % n_rows
    parity = col_index // n_rows
    blocks = matrix.reshape(row_tiles * tile_size, col_tiles * tile_size)
    gathered = lax.all_gather(vectors, "col", axis=3, tiled=True)
    basis_rows = gathered.reshape(panel_count, row_tiles * tile_size, width)
    basis_cols = spread(select_cols(basis_rows, col_tiles, stride, parity), "row", source)
    rows_all = jnp.concatenate([basis_rows[0], basis_rows[1]], axis=1)
    cols_all = jnp.concatenate([basis_cols[0], basis_cols[1]], axis=1)
    image_all = lax.psum(large_product(blocks, cols_all), "col")
    gram_all = lax.psum(contract(rows_all, jnp.concatenate([rows_all, image_all], axis=1)), "row")
    first_gram = gram_all[:width, 2 * width : 3 * width]
    basis_gram = gram_all[:width, width : 2 * width]
    image_gram = gram_all[width : 2 * width, 2 * width : 3 * width].T
    last_gram = gram_all[width : 2 * width, 3 * width :]
    factor_one = factors[0]
    factor_two = factors[1]
    shift_one = 0.5 * product(factor_one.T, product(first_gram, factor_one))
    crossed = product(factor_one.T, image_gram) - product(shift_one.T, basis_gram)
    secondary = last_gram - product(basis_gram.T, crossed) - product(crossed.T, basis_gram)
    shift_two = 0.5 * product(factor_two.T, product(secondary, factor_two))
    basis_one = basis_rows[0]
    update_one = product(image_all[:, :width], factor_one) - product(basis_one, shift_one)
    moved_two = image_all[:, width:] - product(basis_one, crossed) - product(update_one, basis_gram)
    update_two = product(moved_two, factor_two) - product(basis_rows[1], shift_two)
    update_rows = jnp.concatenate([update_one, update_two], axis=1)
    update_cols = spread(select_cols(update_rows, col_tiles, stride, parity), "row", source)
    blocks = rank_update(blocks, rows_all, update_rows, update_cols, cols_all)
    return blocks.reshape(matrix.shape)


def solution(mesh):
    return jax.shard_map(
        shards,
        mesh=mesh,
        in_specs=(P(None, "row", None, None, "col", None), P(None, None, "row", "col", None), P()),
        out_specs=P(None, "row", None, None, "col", None),
        check_vma=False,
    )
```
